32 devices in a mesh: seq: 4 (over y, core), row: 4 (over z), col: 2 (over x).
Axes of the slice: x: 2, y: 2, z: 4, core: 2. Of those that a mesh axis runs over, the one named last changes fastest.
Arguments:
- tokens: bfloat16 [512, 6144], P('seq', 'row'), may hold values from -6 to 6
- weight: bfloat16 [6144, 24576], P('row', 'col'), may hold values from -0.078125 to 0.078125
- cotangent: bfloat16 [512, 24576], P(('seq', 'row'), 'col'), may hold values from -6 to 6
Outputs:
- activation: bfloat16 [512, 24576], P(('seq', 'row'), 'col')
- input_grad: bfloat16 [512, 6144], P('seq', 'row')
- weight_grad: bfloat16 [24576, 6144], P(('col', 'seq'), 'row')
The draws below stay inside these ranges and needn't reach their ends.
All inputs are finite; a program needn't handle non-finite values.
Results may differ from the reference program's by a relative error of at most 0.02.
Values may be sent and summed in bfloat16 or wider, within the bound.
A program may use at most 128 MiB of HBM per device.

```python
import jax
import jax.numpy as jnp
from jax import lax

D = 6144
F = 24576
TOK_SEQ = 128
TOKENS = 512
N_SEQ = 4


def with_spikes(array, rng, source, target, shards_of, factor):
    def block_of(dim):
        return (jnp.arange(array.shape[dim]) // (array.shape[dim] // shards_of)).reshape((-1,) + (1,) * (array.ndim - 1 - dim))

    one_side = jax.random.permutation(rng, shards_of)[block_of(target)]
    other_side = (block_of(target) + shards_of // 2) % shards_of
    return jnp.where((block_of(source) == one_side) | (block_of(source) == other_side), factor * array, array)


def block_scale(own_key, shape, pieces, least, high):
    gain, own = 1.0, jax.random.fold_in(own_key, 6)
    for position, parts in pieces:
        steps = jnp.exp(jax.random.uniform(jax.random.fold_in(own, position), (parts,), jnp.float32, least / len(pieces), high / len(pieces)))
        gain = gain * jnp.repeat(steps, shape[position] // parts).reshape([-1 if axis == position else 1 for axis in range(len(shape))])
    return gain


def scatter_about(stream_key, dims, deviation, most, split=(), held_as=jnp.bfloat16):
    entries = deviation * jax.random.normal(stream_key, dims, jnp.float32)
    if split:
        entries = entries * block_scale(stream_key, dims, split, -0.22, 0.18)
    return jnp.clip(entries, -most, most).astype(held_as)


def heavy_noise(key, shape, deviation, bound, shards, heavy, kind=jnp.bfloat16):
    result = deviation * jax.random.normal(key, shape, jnp.float32)
    if shards:
        result = result * block_scale(key, shape, shards, -0.22, 0.18)
    return jnp.clip(with_spikes(result, jax.random.fold_in(key, 3), *heavy), -bound, bound).astype(kind)


def setup_inputs(seed: int = 0) -> dict:
    arg_keys = jax.random.split(jax.random.key(seed), 4)
    return {
        "tokens": scatter_about(arg_keys[0], (TOKENS, D), 1.0, 6.0, ((0, 4), (1, 4))),
        "weight": scatter_about(arg_keys[1], (D, F), D ** -0.5, 0.078125, ((0, 4), (1, 2))),
        "cotangent": heavy_noise(arg_keys[2], (TOKENS, F), 1.0, 6.0, ((0, 16), (1, 2)), (0, 1, 16, 2.0)),
    }


def gelu_tanh(value):
    return jax.nn.gelu(value, approximate=True)

def reference(tokens, weight, cotangent):
    pre = jnp.dot(tokens, weight, preferred_element_type=jnp.float32)
    active, pull_back = jax.vjp(gelu_tanh, pre)
    activation = active.astype(jnp.bfloat16)
    dpre = pull_back(cotangent.astype(pre.dtype))[0].astype(jnp.bfloat16)
    input_grad = jnp.dot(dpre, weight.T, preferred_element_type=jnp.float32).astype(jnp.bfloat16)
    grad_groups = dpre.reshape(N_SEQ, TOK_SEQ, F)
    token_groups = tokens.reshape(N_SEQ, TOK_SEQ, D)

    def add_group(carry, pair):
        grad_block, token_block = pair
        part = jnp.dot(grad_block.T, token_block, preferred_element_type=jnp.float32).astype(jnp.bfloat16)
        part = lax.optimization_barrier(part)
        return (carry + part.astype(carry.dtype), None)
    total, unused = lax.scan(add_group, jnp.zeros((F, D), jnp.float32), (grad_groups, token_groups))
    return (activation, input_grad, total.astype(jnp.bfloat16))
```

```python
import functools

import jax
import jax.numpy as jnp
from jax import lax
from jax.experimental import pallas as pl
from jax.experimental.pallas import tpu as pltpu
from jax.sharding import PartitionSpec as P

BF, F32 = jnp.bfloat16, jnp.float32
MESH = pl.DeviceIdType.MESH
ROOT = 0.7978845608028654
LAG = 1
PIECES = {1: 3, 2: 2}


def remote(src, dst, send, recv, device):
    return pltpu.make_async_remote_copy(
        src_ref=src, dst_ref=dst, send_sem=send, recv_sem=recv, device_id=device, device_id_type=MESH
    )


def kernel(S, R, NH, Q, *refs):
    outs = 6 if Q > 1 else 4
    tok, w, cot = refs[:3]
    act, dall, tall, ig = refs[3:7]
    (wv, tokv, cotv, part, rbuf, dbuf, abuf, pre, igacc, igown, igs, igr, wsem, loc, tks, tkr, cts, ctr, rss, rsr, ags,
     agr, acs, acr, dsem, tsem, gss, gsr) = refs[3 + outs:31 + outs]
    if Q > 1:
        early, wearly = refs[7:9]
        wst, xs, xr, xsem, wout = refs[31 + outs:]
    s, r, c = lax.axis_index("seq"), lax.axis_index("row"), lax.axis_index("col")
    H = wv.shape[1]
    ck = H // NH
    m = cot.shape[0] // Q
    T, F = tok.shape
    U = R * m
    J = Q * S * NH
    pair = 2 if S % 2 == 0 else 1

    def order(k):
        return jnp.where(k == 0, 0, 1 + k % max(S - 1, 1))

    def owner(k):
        i = order(k)
        return ((s // pair + i // pair) % (S // pair)) * pair + (s + i) % pair

    def reader(k):
        i = order(k)
        return ((s // pair + S // pair - i // pair) % (S // pair)) * pair + (s + i) % pair

    def at(seq=None, row=None, col=None):
        return (s if seq is None else seq, r if row is None else row, c if col is None else col)

    def cols(group, h=0, size=H):
        return pl.ds(pl.multiple_of(group * H + h * ck, 128), size)

    def unit(j):
        u = j // NH
        q, k = u // S, u % S
        if Q > 1:
            k = jnp.where(q == Q - 1, (k + 1) % S, k)
        return q, k, j % NH

    def rows(q):
        return pl.ds(pl.multiple_of(q * m, m), m)

    def tokens_of(k, q):
        if Q == 1:
            return tokv[k]
        return jnp.concatenate(
            [tokv[k, pl.ds(pl.multiple_of((o * Q + q) * m, m), m), :] for o in range(R)], axis=0
        )

    right, left = lax.rem(r + 1, R), lax.rem(r + R - 1, R)

    wcopy = [pltpu.make_async_copy(w.at[:, cols(s, h, ck)], wv.at[:, pl.ds(h * ck, ck)], wsem.at[h]) for h in range(NH)]
    own_tok = pltpu.make_async_copy(tok, tokv.at[0], loc.at[0])
    own_cot = pltpu.make_async_copy(cot.at[:, cols(s)], cotv.at[0], loc.at[1])
    own_tok.start()
    for cp in wcopy:
        cp.start()
    own_cot.start()

    barrier = pltpu.get_barrier_semaphore()

    def greet(device):
        pl.semaphore_signal(barrier, inc=1, device_id=device, device_id_type=MESH)

    for k in range(1, S):
        greet(at(seq=reader(k)))

    @pl.when(r > 0)
    def _():
        greet(at(row=left))

    @pl.when(r < R - 1)
    def _():
        greet(at(row=right))

    if Q > 1:
        greet(at(col=1 - c))

    pl.semaphore_wait(barrier, (S - 1) + (1 if Q > 1 else 0) + jnp.where(r > 0, 1, 0) + jnp.where(r < R - 1, 1, 0))

    def tok_copy(k):
        return remote(tok, tokv.at[k], tks.at[k], tkr.at[k], at(seq=reader(k)))

    def cot_copy(k):
        return remote(cot.at[:, cols(reader(k))], cotv.at[k], cts.at[k], ctr.at[k], at(seq=reader(k)))

    for k in range(1, S):
        tok_copy(k).start()
        cot_copy(k).start()

    def sum_right(j, o):
        return remote(part.at[j, o], rbuf.at[j, o], rss.at[j, o], rsr.at[j, o], at(row=right))

    def sum_left(j, o):
        slot = jnp.where(o == r - 1, R, o)
        return remote(part.at[j, o], rbuf.at[j, slot], rss.at[j, o], rsr.at[j, slot], at(row=left))

    def got_sum(j, slot):
        remote(part.at[j, 0], rbuf.at[j, slot], rss.at[j, 0], rsr.at[j, slot], at(row=right)).wait_recv()

    def d_right(j, o):
        return remote(dbuf.at[j, o], dbuf.at[j, o], ags.at[j, o], agr.at[j, o], at(row=right))

    def d_left(j, o):
        return remote(dbuf.at[j, o], dbuf.at[j, o], ags.at[j, jnp.where(o == r, R, o)], agr.at[j, o], at(row=left))

    def act_remote(j, q, k, h):
        return remote(abuf.at[j], act.at[rows(q), cols(s, h, ck)], acs.at[j], acr.at[j], at(seq=owner(k)))

    def act_local(j, q, h):
        return pltpu.make_async_copy(abuf.at[j], act.at[rows(q), cols(s, h, ck)], acr.at[j])

    def ig_copy(q, k):
        return remote(igs.at[q, k], igr.at[q, k], gss.at[q, k], gsr.at[q, k], at(seq=owner(k)))

    def x_copy():
        return remote(xs, xr, xsem.at[0], xsem.at[1], at(col=1 - c))

    def early_copy(h):
        return pltpu.make_async_copy(
            wst.at[pl.ds(pl.multiple_of(h * ck, 128), ck)], wearly.at[pl.ds(pl.multiple_of(h * ck, 128), ck)], wout.at[h]
        )

    def tall_copy(k, o):
        if Q == 1:
            return pltpu.make_async_copy(tokv.at[k], tall.at[k], tsem.at[k, o])
        return pltpu.make_async_copy(
            tokv.at[k, pl.ds((o * Q + Q - 1) * m, m), :], tall.at[k, pl.ds(o * m, m), :], tsem.at[k, o]
        )

    def dall_copy(j, k, h):
        return pltpu.make_async_copy(dbuf.at[j], dall.at[k, :, :, pl.ds(pl.multiple_of(h * ck, 128), ck)], dsem.at[j])

    def each(n, fn):
        def body(i, carry):
            fn(i)
            return carry
        lax.fori_loop(0, n, body, 0)

    tile = 512 if ck % 512 == 0 else (384 if ck % 384 == 0 else 128)
    ftile = 512 if F % 512 == 0 else 128

    def project(j):
        q, k, h = unit(j)

        @pl.when((q == 0) & (k == 0))
        def _():
            @pl.when(h == 0)
            def _():
                own_tok.wait()
            for i in range(NH):
                @pl.when(h == i)
                def _():
                    wcopy[i].wait()

        @pl.when((q == 0) & (k > 0) & (h == 0))
        def _():
            tok_copy(k).wait_recv()

        @pl.when((q == 0) & (h == 0))
        def _():
            for o in range(R if Q > 1 else 1):
                tall_copy(k, o).start()

        def columns(i):
            here = pl.ds(pl.multiple_of(i * tile, 128), tile)
            there = pl.ds(pl.multiple_of(h * ck + i * tile, 128), tile)
            value = jnp.dot(tokens_of(k, q), wv[:, there], preferred_element_type=F32)
            part[j, :, :, here] = value.reshape(R, m, tile).astype(BF)

        each(ck // tile, columns)

        @pl.when(r == 0)
        def _():
            each(R - 1, lambda i: sum_right(j, R - 1 - i).start())

        @pl.when(r == R - 1)
        def _():
            each(R - 1, lambda i: sum_left(j, i).start())

    def far(o):
        return jnp.maximum(o, R - 1 - o)

    def add_right(j):
        def go(i):
            o = R - 1 - i

            @pl.when(o > r)
            def _():
                got_sum(j, o)
                part[j, o] = (part[j, o].astype(F32) + rbuf[j, o].astype(F32)).astype(BF)
                sum_right(j, o).start()
        each(R - 1, go)

    def add_left(j):
        def go(o):
            @pl.when(o < r)
            def _():
                got_sum(j, o)
                part[j, o] = (part[j, o].astype(F32) + rbuf[j, o].astype(F32)).astype(BF)
                sum_left(j, o).start()
        each(R - 1, go)

    def finish(j):
        q, k, h = unit(j)
        pre[...] = part[j, r].astype(F32)

        @pl.when(r > 0)
        def _():
            got_sum(j, r)
            pre[...] += rbuf[j, r].astype(F32)

        @pl.when(r < R - 1)
        def _():
            got_sum(j, R)
            pre[...] += rbuf[j, R].astype(F32)

        @pl.when((q == 0) & (k == 0) & (h == 0))
        def _():
            own_cot.wait()

        @pl.when((q == 0) & (k > 0) & (h == 0))
        def _():
            cot_copy(k).wait_recv()

        v = pre[...]
        sq = v * v
        t = jnp.tanh(ROOT * (v + 0.044715 * (sq * v)))
        half = 0.5 * (1.0 + t)
        slope = half + 0.5 * v * (1.0 - t * t) * (ROOT * (1.0 + (3 * 0.044715) * sq))
        ct = cotv[k, rows(q), pl.ds(pl.multiple_of(h * ck, 128), ck)].astype(F32)
        dbuf[j, r] = (ct * slope).astype(BF)
        abuf[j] = (v * half).astype(BF)

        @pl.when(r < R - 1)
        def _():
            d_right(j, r).start()

        @pl.when(r > 0)
        def _():
            d_left(j, r).start()

        @pl.when(k == 0)
        def _():
            act_local(j, q, h).start()

        @pl.when(k > 0)
        def _():
            act_remote(j, q, k, h).start()

    def relay(t):
        def go(o):
            j = t - LAG * (far(o) + jnp.abs(r - o))

            @pl.when((o < r) & (j >= 0) & (j < J))
            def _():
                d_right(j, o).wait_recv()

                @pl.when(r < R - 1)
                def _():
                    d_right(j, o).start()

            @pl.when((o > r) & (j >= 0) & (j < J))
            def _():
                d_left(j, o).wait_recv()

                @pl.when(r > 0)
                def _():
                    d_left(j, o).start()

        each(R, go)

    def pull(j):
        q, k, h = unit(j)

        @pl.when(q == Q - 1)
        def _():
            dall_copy(j, k, h).start()

        def features(i):
            here = pl.ds(pl.multiple_of(i * ftile, 128), ftile)
            grads = dbuf[j]
            if m % 16:
                grads = grads.astype(F32)
            grads = grads.reshape(U, ck).astype(BF)
            value = lax.dot_general(
                grads, wv[here, pl.ds(pl.multiple_of(h * ck, 128), ck)], (((1,), (1,)), ((), ())),
                preferred_element_type=F32,
            )

            @pl.when(h == 0)
            def _():
                igacc[:, here] = value

            @pl.when(h > 0)
            def _():
                igacc[:, here] += value

        each(F // ftile, features)

        @pl.when((h == NH - 1) & (k == 0))
        def _():
            igown[q] = igacc[...]

        @pl.when((h == NH - 1) & (k > 0))
        def _():
            igs[q, k] = igacc[...].astype(BF)
            ig_copy(q, k).start()

        if Q > 1:
            @pl.when((q == 0) & (k == S - 1))
            def _():
                partial_grad(h)

            @pl.when((q == Q - 1) & (k == S - 1) & (h == 0))
            def _():
                for i in range(1, S):
                    ig_copy(0, i).wait_recv()
                    igown[0] += igr[0, i].astype(F32)
                xs[...] = igown[0].astype(BF)
                x_copy().start()

    def partial_grad(h):
        def hidden(i):
            here = pl.ds(pl.multiple_of(i * tile, 128), tile)
            there = pl.ds(pl.multiple_of(h * ck + i * tile, 128), tile)
            grads = jnp.concatenate([dbuf[k * NH + h, :, :, here].reshape(U, tile) for k in range(S)], axis=0)
            toks = jnp.concatenate([tokens_of(k, 0) for k in range(S)], axis=0)
            value = lax.dot_general(grads, toks, (((0,), (0,)), ((), ())), preferred_element_type=F32)
            wst[there, :] = value.astype(BF)

        each(ck // tile, hidden)
        early_copy(h).start()

    def at_step(j, ok, fn):
        @pl.when(ok & (j >= 0) & (j < J))
        def _():
            fn(j)

    def step(t):
        at_step(t, True, project)
        at_step(t - LAG * (R - 1 + far(r)) - 1, True, pull)
        at_step(t - LAG * r, r > 0, add_right)
        at_step(t - LAG * (R - 1 - r), r < R - 1, add_left)
        at_step(t - LAG * far(r), True, finish)
        relay(t)

    each(J + LAG * 2 * (R - 1) + 1, step)

    for k in range(1, S):
        ig_copy(Q - 1, k).wait_recv()
        igown[Q - 1] += igr[Q - 1, k].astype(F32)
    ig[...] = igown[Q - 1].astype(BF)
    if Q > 1:
        x_copy().wait_recv()
        early[...] = (xs[...].astype(F32) + xr[...].astype(F32)).astype(BF)
        x_copy().wait_send()
        for h in range(NH):
            early_copy(h).wait()

    for k in range(1, S):
        tok_copy(k).wait_send()
        cot_copy(k).wait_send()
        for q in range(Q):
            ig_copy(q, k).wait_send()
    for k in range(S):
        for o in range(R if Q > 1 else 1):
            tall_copy(k, o).wait()

    def drain(j):
        q, k, h = unit(j)

        @pl.when(q == Q - 1)
        def _():
            dall_copy(j, k, h).wait()

        @pl.when(k == 0)
        def _():
            act_local(j, q, h).wait()

        @pl.when(k > 0)
        def _():
            act_remote(j, q, k, h).wait()

        def block(o):
            @pl.when(o > r)
            def _():
                sum_right(j, o).wait_send()

                @pl.when(r > 0)
                def _():
                    d_left(j, o).wait_send()

            @pl.when(o < r)
            def _():
                sum_left(j, o).wait_send()

                @pl.when(r < R - 1)
                def _():
                    d_right(j, o).wait_send()

        each(R, block)

        @pl.when(r < R - 1)
        def _():
            d_right(j, r).wait_send()

        @pl.when(r > 0)
        def _():
            d_left(j, r).wait_send()

    each(J, drain)


def solution(mesh):
    S, R, C = (mesh.shape[name] for name in ("seq", "row", "col"))

    def shards(tokens, weight, cotangent):
        T, F = tokens.shape
        H = weight.shape[1] // S
        Q = 2 if C == 2 and S > 2 and cotangent.shape[0] % 32 == 0 else 1
        m = cotangent.shape[0] // Q
        U = R * m
        NH = next(n for n in (PIECES[Q], 1) if n == 1 or (H % (n * 128) == 0 and H >= 512 * n))
        J, ck = Q * S * NH, H // NH
        dma = pltpu.SemaphoreType.DMA
        anywhere = pl.BlockSpec(memory_space=pl.ANY)
        inside = pl.BlockSpec(memory_space=pltpu.VMEM)
        out_shape = [
            jax.ShapeDtypeStruct((Q * m, S * H), BF),
            jax.ShapeDtypeStruct((S, R, m, H), BF),
            jax.ShapeDtypeStruct((S, U, F), BF),
            jax.ShapeDtypeStruct((U, F), BF),
        ]
        out_specs = [anywhere, anywhere, anywhere, inside]
        scratch = [
            pltpu.VMEM((F, H), BF),
            pltpu.VMEM((S, T, F), BF),
            pltpu.VMEM((S, Q * m, H), BF),
            pltpu.VMEM((J, R, m, ck), BF),
            pltpu.VMEM((J, R + 1, m, ck), BF),
            pltpu.VMEM((J, R, m, ck), BF),
            pltpu.VMEM((J, m, ck), BF),
            pltpu.VMEM((m, ck), F32),
            pltpu.VMEM((U, F), F32),
            pltpu.VMEM((Q, U, F), F32),
            pltpu.VMEM((Q, S, U, F), BF),
            pltpu.VMEM((Q, S, U, F), BF),
            dma((NH,)),
            dma((2,)),
            dma((S,)), dma((S,)), dma((S,)), dma((S,)),
            dma((J, R)), dma((J, R + 1)), dma((J, R + 1)), dma((J, R)),
            dma((J,)), dma((J,)), dma((J,)), dma((S, R)),
            dma((Q, S)), dma((Q, S)),
        ]
        if Q > 1:
            out_shape += [jax.ShapeDtypeStruct((U, F), BF), jax.ShapeDtypeStruct((H, F), BF)]
            out_specs += [inside, anywhere]
            scratch += [
                pltpu.VMEM((H, F), BF), pltpu.VMEM((U, F), BF), pltpu.VMEM((U, F), BF), dma((2,)), dma((NH,)),
            ]
        act, dall, tall, ig, *more = pl.pallas_call(
            functools.partial(kernel, S, R, NH, Q),
            out_shape=tuple(out_shape),
            in_specs=[anywhere] * 3,
            out_specs=tuple(out_specs),
            scratch_shapes=scratch,
            compiler_params=pltpu.CompilerParams(
                collective_id=0, has_side_effects=True, vmem_limit_bytes=60 * 1024 * 1024
            ),
        )(tokens, weight, cotangent)
        if C == 2:
            other = lax.ppermute(ig, "col", [(0, 1), (1, 0)])
            total = (ig.astype(F32) + other.astype(F32)).astype(BF)
        else:
            total = lax.psum(ig, "col")
        grad = lax.dot_general(
            dall.reshape(S * U, H), tall.reshape(S * U, F), (((0,), (0,)), ((), ())), preferred_element_type=F32
        )
        if Q > 1:
            total = jnp.stack([more[0].reshape(R, m, F), total.reshape(R, m, F)], axis=1).reshape(T, F)
            grad = grad + more[1].astype(F32)
        return act, total, grad.astype(BF)

    in_specs = (P("seq", "row"), P("row", "col"), P(("seq", "row"), "col"))
    out_specs = (P(("seq", "row"), "col"), P("seq", "row"), P(("col", "seq"), "row"))
    return jax.shard_map(shards, mesh=mesh, in_specs=in_specs, out_specs=out_specs, check_vma=False)
```

```python
import functools

import jax
import jax.numpy as jnp
from jax import lax
from jax.experimental import pallas as pl
from jax.experimental.pallas import tpu as pltpu
from jax.sharding import PartitionSpec as P

BF, F32 = jnp.bfloat16, jnp.float32
MESH = pl.DeviceIdType.MESH
ROOT = 0.7978845608028654
LAG = 1


def remote(src, dst, send, recv, device):
    return pltpu.make_async_remote_copy(
        src_ref=src, dst_ref=dst, send_sem=send, recv_sem=recv, device_id=device, device_id_type=MESH
    )


def kernel(S, R, NH, tok, w, cot, act, dall, tall, ig, wv, tokv, cotv, part, rbuf, dbuf, abuf, pre, igacc, igown,
           igs, igr, wsem, loc, tks, tkr, cts, ctr, rss, rsr, ags, agr, acs, acr, dsem, tsem, gss, gsr):
    s, r, c = lax.axis_index("seq"), lax.axis_index("row"), lax.axis_index("col")
    H = wv.shape[1]
    ck = H // NH
    m = cot.shape[0]
    T, F = tok.shape
    J = S * NH
    pair = 2 if S % 2 == 0 else 1

    def order(k):
        return jnp.where(k == 0, 0, 1 + k % max(S - 1, 1))

    def owner(k):
        i = order(k)
        return ((s // pair + i // pair) % (S // pair)) * pair + (s + i) % pair

    def reader(k):
        i = order(k)
        return ((s // pair + S // pair - i // pair) % (S // pair)) * pair + (s + i) % pair

    def at(seq=None, row=None, col=None):
        return (s if seq is None else seq, r if row is None else row, c if col is None else col)

    def cols(group, h=0, size=H):
        return pl.ds(pl.multiple_of(group * H + h * ck, 128), size)

    def unit(j):
        if NH == 1:
            return j, 0
        e = j - (NH - 1)
        mine = (e < 0) | (e >= (S - 1) * NH)
        k = jnp.where(mine, 0, 1 + jnp.maximum(e, 0) // NH)
        return k, jnp.where(mine, jnp.where(e < 0, j, NH - 1), jnp.maximum(e, 0) % NH)

    right, left = lax.rem(r + 1, R), lax.rem(r + R - 1, R)

    wcopy = [pltpu.make_async_copy(w.at[:, cols(s, h, ck)], wv.at[:, pl.ds(h * ck, ck)], wsem.at[h]) for h in range(NH)]
    own_tok = pltpu.make_async_copy(tok, tokv.at[0], loc.at[0])
    own_cot = pltpu.make_async_copy(cot.at[:, cols(s)], cotv.at[0], loc.at[1])
    own_tok.start()
    for cp in wcopy:
        cp.start()
    own_cot.start()

    barrier = pltpu.get_barrier_semaphore()

    def greet(device):
        pl.semaphore_signal(barrier, inc=1, device_id=device, device_id_type=MESH)

    for k in range(1, S):
        greet(at(seq=reader(k)))

    @pl.when(r > 0)
    def _():
        greet(at(row=left))

    @pl.when(r < R - 1)
    def _():
        greet(at(row=right))

    pl.semaphore_wait(barrier, (S - 1) + jnp.where(r > 0, 1, 0) + jnp.where(r < R - 1, 1, 0))

    def tok_copy(k):
        return remote(tok, tokv.at[k], tks.at[k], tkr.at[k], at(seq=reader(k)))

    def cot_copy(k):
        return remote(cot.at[:, cols(reader(k))], cotv.at[k], cts.at[k], ctr.at[k], at(seq=reader(k)))

    for k in range(1, S):
        tok_copy(k).start()
        cot_copy(k).start()

    def sum_right(j, o):
        return remote(part.at[j, o], rbuf.at[j, o], rss.at[j, o], rsr.at[j, o], at(row=right))

    def sum_left(j, o):
        slot = jnp.where(o == r - 1, R, o)
        return remote(part.at[j, o], rbuf.at[j, slot], rss.at[j, o], rsr.at[j, slot], at(row=left))

    def got_sum(j, slot):
        remote(part.at[j, 0], rbuf.at[j, slot], rss.at[j, 0], rsr.at[j, slot], at(row=right)).wait_recv()

    def d_right(j, o):
        return remote(dbuf.at[j, o], dbuf.at[j, o], ags.at[j, o], agr.at[j, o], at(row=right))

    def d_left(j, o):
        return remote(dbuf.at[j, o], dbuf.at[j, o], ags.at[j, jnp.where(o == r, R, o)], agr.at[j, o], at(row=left))

    def act_remote(j, k, h):
        return remote(abuf.at[j], act.at[:, cols(s, h, ck)], acs.at[j], acr.at[j], at(seq=owner(k)))

    def act_local(j, h):
        return pltpu.make_async_copy(abuf.at[j], act.at[:, cols(s, h, ck)], acr.at[j])

    def ig_copy(k):
        return remote(igs.at[k], igr.at[k], gss.at[k], gsr.at[k], at(seq=owner(k)))

    def tall_copy(k):
        return pltpu.make_async_copy(tokv.at[k], tall.at[k], tsem.at[k])

    def dall_copy(j, k, h):
        return pltpu.make_async_copy(dbuf.at[j], dall.at[k, :, :, pl.ds(pl.multiple_of(h * ck, 128), ck)], dsem.at[j])

    def each(n, fn):
        def body(i, carry):
            fn(i)
            return carry
        lax.fori_loop(0, n, body, 0)

    tile = 512 if ck % 512 == 0 else (384 if ck % 384 == 0 else 128)
    ftile = 512 if F % 512 == 0 else 128

    def project(j):
        k, h = unit(j)

        @pl.when((k == 0) & (h == 0))
        def _():
            own_tok.wait()

        for i in range(NH):
            @pl.when((k == (1 if i and i == NH - 1 else 0)) & (h == i))
            def _():
                wcopy[i].wait()

        @pl.when((k > 0) & (h == 0))
        def _():
            tok_copy(k).wait_recv()

        @pl.when(h == 0)
        def _():
            tall_copy(k).start()

        def columns(i):
            here = pl.ds(pl.multiple_of(i * tile, 128), tile)
            there = pl.ds(pl.multiple_of(h * ck + i * tile, 128), tile)
            value = jnp.dot(tokv[k], wv[:, there], preferred_element_type=F32)
            part[j, :, :, here] = value.reshape(R, m, tile).astype(BF)

        each(ck // tile, columns)

        @pl.when(r == 0)
        def _():
            each(R - 1, lambda i: sum_right(j, R - 1 - i).start())

        @pl.when(r == R - 1)
        def _():
            each(R - 1, lambda i: sum_left(j, i).start())

    def far(o):
        return jnp.maximum(o, R - 1 - o)

    def add_right(j):
        def go(i):
            o = R - 1 - i

            @pl.when(o > r)
            def _():
                got_sum(j, o)
                part[j, o] = (part[j, o].astype(F32) + rbuf[j, o].astype(F32)).astype(BF)
                sum_right(j, o).start()
        each(R - 1, go)

    def add_left(j):
        def go(o):
            @pl.when(o < r)
            def _():
                got_sum(j, o)
                part[j, o] = (part[j, o].astype(F32) + rbuf[j, o].astype(F32)).astype(BF)
                sum_left(j, o).start()
        each(R - 1, go)

    def finish(j):
        k, h = unit(j)
        pre[...] = part[j, r].astype(F32)

        @pl.when(r > 0)
        def _():
            got_sum(j, r)
            pre[...] += rbuf[j, r].astype(F32)

        @pl.when(r < R - 1)
        def _():
            got_sum(j, R)
            pre[...] += rbuf[j, R].astype(F32)

        @pl.when((k == 0) & (h == 0))
        def _():
            own_cot.wait()

        @pl.when((k > 0) & (h == 0))
        def _():
            cot_copy(k).wait_recv()

        v = pre[...]
        sq = v * v
        t = jnp.tanh(ROOT * (v + 0.044715 * (sq * v)))
        half = 0.5 * (1.0 + t)
        slope = half + 0.5 * v * (1.0 - t * t) * (ROOT * (1.0 + (3 * 0.044715) * sq))
        ct = cotv[k, :, pl.ds(pl.multiple_of(h * ck, 128), ck)].astype(F32)
        dbuf[j, r] = (ct * slope).astype(BF)
        abuf[j] = (v * half).astype(BF)

        @pl.when(r < R - 1)
        def _():
            d_right(j, r).start()

        @pl.when(r > 0)
        def _():
            d_left(j, r).start()

        @pl.when(k == 0)
        def _():
            act_local(j, h).start()

        @pl.when(k > 0)
        def _():
            act_remote(j, k, h).start()

    def relay(t):
        def go(o):
            j = t - LAG * (far(o) + jnp.abs(r - o))

            @pl.when((o < r) & (j >= 0) & (j < J))
            def _():
                d_right(j, o).wait_recv()

                @pl.when(r < R - 1)
                def _():
                    d_right(j, o).start()

            @pl.when((o > r) & (j >= 0) & (j < J))
            def _():
                d_left(j, o).wait_recv()

                @pl.when(r > 0)
                def _():
                    d_left(j, o).start()

        each(R, go)

    def pull(j):
        k, h = unit(j)
        dall_copy(j, k, h).start()

        def features(i):
            here = pl.ds(pl.multiple_of(i * ftile, 128), ftile)
            grads = dbuf[j]
            if m % 16:
                grads = grads.astype(F32)
            grads = grads.reshape(R * m, ck).astype(BF)
            value = lax.dot_general(
                grads, wv[here, pl.ds(pl.multiple_of(h * ck, 128), ck)], (((1,), (1,)), ((), ())),
                preferred_element_type=F32,
            )

            @pl.when((k == 0) & (h == 0))
            def _():
                igown[:, here] = value

            @pl.when((k == 0) & (h > 0))
            def _():
                igown[:, here] += value

            @pl.when((k > 0) & (h == 0))
            def _():
                igacc[:, here] = value

            @pl.when((k > 0) & (h > 0))
            def _():
                igacc[:, here] += value

        each(F // ftile, features)

        @pl.when((h == NH - 1) & (k > 0))
        def _():
            igs[k] = igacc[...].astype(BF)
            ig_copy(k).start()

        @pl.when((h == NH - 1) & (k == S - 1))
        def _():
            for i in range(1, S - 1):
                ig_copy(i).wait_recv()
                igown[...] += igr[i].astype(F32)

    def at_step(j, ok, fn):
        @pl.when(ok & (j >= 0) & (j < J))
        def _():
            fn(j)

    def step(t):
        at_step(t, True, project)
        at_step(t - LAG * (R - 1 + far(r)) - 1, True, pull)
        at_step(t - LAG * r, r > 0, add_right)
        at_step(t - LAG * (R - 1 - r), r < R - 1, add_left)
        at_step(t - LAG * far(r), True, finish)
        relay(t)

    each(J + LAG * 2 * (R - 1) + 1, step)

    ig_copy(S - 1).wait_recv()
    ig[...] = (igown[...] + igr[S - 1].astype(F32)).astype(BF)

    for k in range(1, S):
        tok_copy(k).wait_send()
        cot_copy(k).wait_send()
        ig_copy(k).wait_send()
    for k in range(S):
        tall_copy(k).wait()

    def drain(j):
        k, h = unit(j)
        dall_copy(j, k, h).wait()

        @pl.when(k == 0)
        def _():
            act_local(j, h).wait()

        @pl.when(k > 0)
        def _():
            act_remote(j, k, h).wait()

        def block(o):
            @pl.when(o > r)
            def _():
                sum_right(j, o).wait_send()

                @pl.when(r > 0)
                def _():
                    d_left(j, o).wait_send()

            @pl.when(o < r)
            def _():
                sum_left(j, o).wait_send()

                @pl.when(r < R - 1)
                def _():
                    d_right(j, o).wait_send()

        each(R, block)

        @pl.when(r < R - 1)
        def _():
            d_right(j, r).wait_send()

        @pl.when(r > 0)
        def _():
            d_left(j, r).wait_send()

    each(J, drain)


def weight_kernel(sub, grads, toks, act, grad, act_out):
    act_out[...] = act[...]

    def go(i, carry):
        here = pl.ds(pl.multiple_of(i * sub, 128), sub)
        grad[:, here] = lax.dot_general(
            grads[...], toks[:, here], (((0,), (0,)), ((), ())), preferred_element_type=F32
        ).astype(BF)
        return carry

    lax.fori_loop(0, grad.shape[1] // sub, go, 0)


def weight_grad(grads, toks, act):
    K, H = grads.shape
    F = toks.shape[1]
    m, width = act.shape
    tm = next(n for n in (512, 384, 128) if H % n == 0)
    n = H // tm
    return pl.pallas_call(
        functools.partial(weight_kernel, F),
        out_shape=(jax.ShapeDtypeStruct((H, F), BF), jax.ShapeDtypeStruct((m, width), BF)),
        grid=(n,),
        in_specs=[
            pl.BlockSpec((K, tm), lambda i: (0, i)),
            pl.BlockSpec((K, F), lambda i: (0, 0), pipeline_mode=pl.Buffered(1)),
            pl.BlockSpec((m, width // n), lambda i: (0, i)),
        ],
        out_specs=(pl.BlockSpec((tm, F), lambda i: (i, 0)), pl.BlockSpec((m, width // n), lambda i: (0, i))),
        compiler_params=pltpu.CompilerParams(vmem_limit_bytes=24 * 1024 * 1024),
        cost_estimate=pl.CostEstimate(
            flops=2 * K * H * F, bytes_accessed=2 * (K * H + K * F + H * F + 2 * m * width), transcendentals=0
        ),
    )(grads, toks, act)


def solution(mesh):
    S, R, C = (mesh.shape[name] for name in ("seq", "row", "col"))

    def shards(tokens, weight, cotangent):
        T, F = tokens.shape
        H = weight.shape[1] // S
        m = cotangent.shape[0]
        NH = next(n for n in (4, 1) if n == 1 or (H % (n * 128) == 0 and H >= 512 * n))
        J, ck = S * NH, H // NH
        dma = pltpu.SemaphoreType.DMA
        anywhere = pl.BlockSpec(memory_space=pl.ANY)
        act, dall, tall, ig = pl.pallas_call(
            functools.partial(kernel, S, R, NH),
            out_shape=(
                jax.ShapeDtypeStruct((m, S * H), BF),
                jax.ShapeDtypeStruct((S, R, m, H), BF),
                jax.ShapeDtypeStruct((S, T, F), BF),
                jax.ShapeDtypeStruct((T, F), BF),
            ),
            in_specs=[anywhere] * 3,
            out_specs=(anywhere, anywhere, anywhere, pl.BlockSpec(memory_space=pltpu.VMEM)),
            scratch_shapes=[
                pltpu.VMEM((F, H), BF),
                pltpu.VMEM((S, T, F), BF),
                pltpu.VMEM((S, m, H), BF),
                pltpu.VMEM((J, R, m, ck), BF),
                pltpu.VMEM((J, R + 1, m, ck), BF),
                pltpu.VMEM((J, R, m, ck), BF),
                pltpu.VMEM((J, m, ck), BF),
                pltpu.VMEM((m, ck), F32),
                pltpu.VMEM((T, F), F32),
                pltpu.VMEM((T, F), F32),
                pltpu.VMEM((S, T, F), BF),
                pltpu.VMEM((S, T, F), BF),
                dma((NH,)),
                dma((2,)),
                dma((S,)), dma((S,)), dma((S,)), dma((S,)),
                dma((J, R)), dma((J, R + 1)), dma((J, R + 1)), dma((J, R)),
                dma((J,)), dma((J,)), dma((J,)), dma((S,)),
                dma((S,)), dma((S,)),
            ],
            compiler_params=pltpu.CompilerParams(
                collective_id=0, has_side_effects=True, vmem_limit_bytes=40 * 1024 * 1024
            ),
        )(*[pltpu.with_memory_space_constraint(x, pltpu.HBM) for x in (tokens, weight, cotangent)])
        if C == 2:
            other = lax.ppermute(ig, "col", [(0, 1), (1, 0)])
            total = (ig.astype(F32) + other.astype(F32)).astype(BF)
        else:
            total = lax.psum(ig, "col")
        grad, act = weight_grad(dall.reshape(S * T, H), tall.reshape(S * T, F), act)
        return act, total, grad

    in_specs = (P("seq", "row"), P("row", "col"), P(("seq", "row"), "col"))
    out_specs = (P(("seq", "row"), "col"), P("seq", "row"), P(("col", "seq"), "row"))
    return jax.shard_map(shards, mesh=mesh, in_specs=in_specs, out_specs=out_specs, check_vma=False)
```

```python
import functools

import jax
import jax.numpy as jnp
from jax import lax
from jax.experimental import pallas as pl
from jax.experimental.pallas import tpu as pltpu
from jax.sharding import PartitionSpec as P

BF, F32 = jnp.bfloat16, jnp.float32
MESH = pl.DeviceIdType.MESH
ROOT = 0.7978845608028654
LAG = 1


def remote(src, dst, send, recv, device):
    return pltpu.make_async_remote_copy(
        src_ref=src, dst_ref=dst, send_sem=send, recv_sem=recv, device_id=device, device_id_type=MESH
    )


def kernel(S, R, NH, tok, w, cot, act, dall, tall, ig, wv, tokv, cotv, part, rbuf, dbuf, abuf, pre, igacc, igown,
           igs, igr, wsem, loc, tks, tkr, cts, ctr, rss, rsr, ags, agr, acs, acr, dsem, tsem, gss, gsr):
    s, r, c = lax.axis_index("seq"), lax.axis_index("row"), lax.axis_index("col")
    H = wv.shape[1]
    ck = H // NH
    m = cot.shape[0]
    T, F = tok.shape
    J = S * NH
    pair = 2 if S % 2 == 0 else 1

    def order(k):
        return jnp.where(k == 0, 0, 1 + k % max(S - 1, 1))

    def owner(k):
        i = order(k)
        return ((s // pair + i // pair) % (S // pair)) * pair + (s + i) % pair

    def reader(k):
        i = order(k)
        return ((s // pair + S // pair - i // pair) % (S // pair)) * pair + (s + i) % pair

    def at(seq=None, row=None, col=None):
        return (s if seq is None else seq, r if row is None else row, c if col is None else col)

    def cols(group, h=0, size=H):
        return pl.ds(pl.multiple_of(group * H + h * ck, 128), size)

    def unit(j):
        if NH == 1:
            return j, 0
        e = j - (NH - 1)
        mine = (e < 0) | (e >= (S - 1) * NH)
        k = jnp.where(mine, 0, 1 + jnp.maximum(e, 0) // NH)
        return k, jnp.where(mine, jnp.where(e < 0, j, NH - 1), jnp.maximum(e, 0) % NH)

    right, left = lax.rem(r + 1, R), lax.rem(r + R - 1, R)

    wcopy = [pltpu.make_async_copy(w.at[:, cols(s, h, ck)], wv.at[:, pl.ds(h * ck, ck)], wsem.at[h]) for h in range(NH)]
    own_tok = pltpu.make_async_copy(tok, tokv.at[0], loc.at[0])
    own_cot = pltpu.make_async_copy(cot.at[:, cols(s)], cotv.at[0], loc.at[1])
    own_tok.start()
    for cp in wcopy:
        cp.start()
    own_cot.start()

    barrier = pltpu.get_barrier_semaphore()

    def greet(device):
        pl.semaphore_signal(barrier, inc=1, device_id=device, device_id_type=MESH)

    for k in range(1, S):
        greet(at(seq=reader(k)))

    @pl.when(r > 0)
    def _():
        greet(at(row=left))

    @pl.when(r < R - 1)
    def _():
        greet(at(row=right))

    pl.semaphore_wait(barrier, (S - 1) + jnp.where(r > 0, 1, 0) + jnp.where(r < R - 1, 1, 0))

    def tok_copy(k):
        return remote(tok, tokv.at[k], tks.at[k], tkr.at[k], at(seq=reader(k)))

    def cot_copy(k):
        return remote(cot.at[:, cols(reader(k))], cotv.at[k], cts.at[k], ctr.at[k], at(seq=reader(k)))

    for k in range(1, S):
        tok_copy(k).start()
        cot_copy(k).start()

    def sum_right(j, o):
        return remote(part.at[j, o], rbuf.at[j, o], rss.at[j, o], rsr.at[j, o], at(row=right))

    def sum_left(j, o):
        slot = jnp.where(o == r - 1, R, o)
        return remote(part.at[j, o], rbuf.at[j, slot], rss.at[j, o], rsr.at[j, slot], at(row=left))

    def got_sum(j, slot):
        remote(part.at[j, 0], rbuf.at[j, slot], rss.at[j, 0], rsr.at[j, slot], at(row=right)).wait_recv()

    def d_right(j, o):
        return remote(dbuf.at[j, o], dbuf.at[j, o], ags.at[j, o], agr.at[j, o], at(row=right))

    def d_left(j, o):
        return remote(dbuf.at[j, o], dbuf.at[j, o], ags.at[j, jnp.where(o == r, R, o)], agr.at[j, o], at(row=left))

    def act_remote(j, k, h):
        return remote(abuf.at[j], act.at[:, cols(s, h, ck)], acs.at[j], acr.at[j], at(seq=owner(k)))

    def act_local(j, h):
        return pltpu.make_async_copy(abuf.at[j], act.at[:, cols(s, h, ck)], acr.at[j])

    def ig_copy(k):
        return remote(igs.at[k], igr.at[k], gss.at[k], gsr.at[k], at(seq=owner(k)))

    def tall_copy(k):
        return pltpu.make_async_copy(tokv.at[k], tall.at[k], tsem.at[k])

    def dall_copy(j, k, h):
        return pltpu.make_async_copy(dbuf.at[j], dall.at[k, :, :, pl.ds(pl.multiple_of(h * ck, 128), ck)], dsem.at[j])

    def each(n, fn):
        def body(i, carry):
            fn(i)
            return carry
        lax.fori_loop(0, n, body, 0)

    tile = 512 if ck % 512 == 0 else (384 if ck % 384 == 0 else 128)
    ftile = 512 if F % 512 == 0 else 128

    def project(j):
        k, h = unit(j)

        @pl.when((k == 0) & (h == 0))
        def _():
            own_tok.wait()

        for i in range(NH):
            @pl.when((k == (1 if i and i == NH - 1 else 0)) & (h == i))
            def _():
                wcopy[i].wait()

        @pl.when((k > 0) & (h == 0))
        def _():
            tok_copy(k).wait_recv()

        @pl.when(h == 0)
        def _():
            tall_copy(k).start()

        def columns(i):
            here = pl.ds(pl.multiple_of(i * tile, 128), tile)
            there = pl.ds(pl.multiple_of(h * ck + i * tile, 128), tile)
            value = jnp.dot(tokv[k], wv[:, there], preferred_element_type=F32)
            part[j, :, :, here] = value.reshape(R, m, tile).astype(BF)

        each(ck // tile, columns)

        @pl.when(r == 0)
        def _():
            each(R - 1, lambda i: sum_right(j, R - 1 - i).start())

        @pl.when(r == R - 1)
        def _():
            each(R - 1, lambda i: sum_left(j, i).start())

    def far(o):
        return jnp.maximum(o, R - 1 - o)

    def add_right(j):
        def go(i):
            o = R - 1 - i

            @pl.when(o > r)
            def _():
                got_sum(j, o)
                part[j, o] = (part[j, o].astype(F32) + rbuf[j, o].astype(F32)).astype(BF)
                sum_right(j, o).start()
        each(R - 1, go)

    def add_left(j):
        def go(o):
            @pl.when(o < r)
            def _():
                got_sum(j, o)
                part[j, o] = (part[j, o].astype(F32) + rbuf[j, o].astype(F32)).astype(BF)
                sum_left(j, o).start()
        each(R - 1, go)

    def finish(j):
        k, h = unit(j)
        pre[...] = part[j, r].astype(F32)

        @pl.when(r > 0)
        def _():
            got_sum(j, r)
            pre[...] += rbuf[j, r].astype(F32)

        @pl.when(r < R - 1)
        def _():
            got_sum(j, R)
            pre[...] += rbuf[j, R].astype(F32)

        @pl.when((k == 0) & (h == 0))
        def _():
            own_cot.wait()

        @pl.when((k > 0) & (h == 0))
        def _():
            cot_copy(k).wait_recv()

        v = pre[...]
        sq = v * v
        t = jnp.tanh(ROOT * (v + 0.044715 * (sq * v)))
        half = 0.5 * (1.0 + t)
        slope = half + 0.5 * v * (1.0 - t * t) * (ROOT * (1.0 + (3 * 0.044715) * sq))
        ct = cotv[k, :, pl.ds(pl.multiple_of(h * ck, 128), ck)].astype(F32)
        dbuf[j, r] = (ct * slope).astype(BF)
        abuf[j] = (v * half).astype(BF)

        @pl.when(r < R - 1)
        def _():
            d_right(j, r).start()

        @pl.when(r > 0)
        def _():
            d_left(j, r).start()

        @pl.when(k == 0)
        def _():
            act_local(j, h).start()

        @pl.when(k > 0)
        def _():
            act_remote(j, k, h).start()

    def relay(t):
        def go(o):
            j = t - LAG * (far(o) + jnp.abs(r - o))

            @pl.when((o < r) & (j >= 0) & (j < J))
            def _():
                d_right(j, o).wait_recv()

                @pl.when(r < R - 1)
                def _():
                    d_right(j, o).start()

            @pl.when((o > r) & (j >= 0) & (j < J))
            def _():
                d_left(j, o).wait_recv()

                @pl.when(r > 0)
                def _():
                    d_left(j, o).start()

        each(R, go)

    def pull(j):
        k, h = unit(j)
        dall_copy(j, k, h).start()

        def features(i):
            here = pl.ds(pl.multiple_of(i * ftile, 128), ftile)
            grads = dbuf[j]
            if m % 16:
                grads = grads.astype(F32)
            grads = grads.reshape(R * m, ck).astype(BF)
            value = lax.dot_general(
                grads, wv[here, pl.ds(pl.multiple_of(h * ck, 128), ck)], (((1,), (1,)), ((), ())),
                preferred_element_type=F32,
            )

            @pl.when((k == 0) & (h == 0))
            def _():
                igown[:, here] = value

            @pl.when((k == 0) & (h > 0))
            def _():
                igown[:, here] += value

            @pl.when((k > 0) & (h == 0))
            def _():
                igacc[:, here] = value

            @pl.when((k > 0) & (h > 0))
            def _():
                igacc[:, here] += value

        each(F // ftile, features)

        @pl.when((h == NH - 1) & (k > 0))
        def _():
            igs[k] = igacc[...].astype(BF)
            ig_copy(k).start()

        @pl.when((h == NH - 1) & (k == S - 1))
        def _():
            for i in range(1, S - 1):
                ig_copy(i).wait_recv()
                igown[...] += igr[i].astype(F32)

    def drain(j):
        k, h = unit(j)
        dall_copy(j, k, h).wait()

        @pl.when(k == 0)
        def _():
            act_local(j, h).wait()

        @pl.when(k > 0)
        def _():
            act_remote(j, k, h).wait()

        def block(o):
            @pl.when(o > r)
            def _():
                sum_right(j, o).wait_send()

                @pl.when(r > 0)
                def _():
                    d_left(j, o).wait_send()

            @pl.when(o < r)
            def _():
                sum_left(j, o).wait_send()

                @pl.when(r < R - 1)
                def _():
                    d_right(j, o).wait_send()

        each(R, block)

        @pl.when(r < R - 1)
        def _():
            d_right(j, r).wait_send()

        @pl.when(r > 0)
        def _():
            d_left(j, r).wait_send()

    def at_step(j, ok, fn):
        @pl.when(ok & (j >= 0) & (j < J))
        def _():
            fn(j)

    def step(t):
        at_step(t, True, project)
        at_step(t - LAG * (R - 1 + far(r)) - 1, True, pull)
        at_step(t - LAG * r, r > 0, add_right)
        at_step(t - LAG * (R - 1 - r), r < R - 1, add_left)
        at_step(t - LAG * far(r), True, finish)
        relay(t)
        at_step(t - LAG * 2 * (R - 1) - 3, True, drain)

    each(J + LAG * 2 * (R - 1) + 1, step)

    ig_copy(S - 1).wait_recv()
    ig[...] = (igown[...] + igr[S - 1].astype(F32)).astype(BF)

    for k in range(1, S):
        tok_copy(k).wait_send()
        cot_copy(k).wait_send()
        ig_copy(k).wait_send()
    for k in range(S):
        tall_copy(k).wait()

    done = max(J - 2, 0)
    each(J - done, lambda i: drain(done + i))


def weight_kernel(sub, grads, toks, act, grad, act_out):
    act_out[...] = act[...]

    def go(i, carry):
        here = pl.ds(pl.multiple_of(i * sub, 128), sub)
        grad[:, here] = lax.dot_general(
            grads[...], toks[:, here], (((0,), (0,)), ((), ())), preferred_element_type=F32
        ).astype(BF)
        return carry

    lax.fori_loop(0, grad.shape[1] // sub, go, 0)


def weight_grad(grads, toks, act):
    K, H = grads.shape
    F = toks.shape[1]
    m, width = act.shape
    tm = next(n for n in (512, 384, 128) if H % n == 0)
    n = H // tm
    return pl.pallas_call(
        functools.partial(weight_kernel, F),
        out_shape=(jax.ShapeDtypeStruct((H, F), BF), jax.ShapeDtypeStruct((m, width), BF)),
        grid=(n,),
        in_specs=[
            pl.BlockSpec((K, tm), lambda i: (0, i)),
            pl.BlockSpec((K, F), lambda i: (0, 0), pipeline_mode=pl.Buffered(1)),
            pl.BlockSpec((m, width // n), lambda i: (0, i)),
        ],
        out_specs=(pl.BlockSpec((tm, F), lambda i: (i, 0)), pl.BlockSpec((m, width // n), lambda i: (0, i))),
        compiler_params=pltpu.CompilerParams(vmem_limit_bytes=24 * 1024 * 1024),
        cost_estimate=pl.CostEstimate(
            flops=2 * K * H * F, bytes_accessed=2 * (K * H + K * F + H * F + 2 * m * width), transcendentals=0
        ),
    )(grads, toks, act)


def solution(mesh):
    S, R, C = (mesh.shape[name] for name in ("seq", "row", "col"))

    def shards(tokens, weight, cotangent):
        T, F = tokens.shape
        H = weight.shape[1] // S
        m = cotangent.shape[0]
        NH = next(n for n in (4, 1) if n == 1 or (H % (n * 128) == 0 and H >= 512 * n))
        J, ck = S * NH, H // NH
        dma = pltpu.SemaphoreType.DMA
        anywhere = pl.BlockSpec(memory_space=pl.ANY)
        act, dall, tall, ig = pl.pallas_call(
            functools.partial(kernel, S, R, NH),
            out_shape=(
                jax.ShapeDtypeStruct((m, S * H), BF),
                jax.ShapeDtypeStruct((S, R, m, H), BF),
                jax.ShapeDtypeStruct((S, T, F), BF),
                jax.ShapeDtypeStruct((T, F), BF),
            ),
            in_specs=[anywhere] * 3,
            out_specs=(anywhere, anywhere, anywhere, pl.BlockSpec(memory_space=pltpu.VMEM)),
            scratch_shapes=[
                pltpu.VMEM((F, H), BF),
                pltpu.VMEM((S, T, F), BF),
                pltpu.VMEM((S, m, H), BF),
                pltpu.VMEM((J, R, m, ck), BF),
                pltpu.VMEM((J, R + 1, m, ck), BF),
                pltpu.VMEM((J, R, m, ck), BF),
                pltpu.VMEM((J, m, ck), BF),
                pltpu.VMEM((m, ck), F32),
                pltpu.VMEM((T, F), F32),
                pltpu.VMEM((T, F), F32),
                pltpu.VMEM((S, T, F), BF),
                pltpu.VMEM((S, T, F), BF),
                dma((NH,)),
                dma((2,)),
                dma((S,)), dma((S,)), dma((S,)), dma((S,)),
                dma((J, R)), dma((J, R + 1)), dma((J, R + 1)), dma((J, R)),
                dma((J,)), dma((J,)), dma((J,)), dma((S,)),
                dma((S,)), dma((S,)),
            ],
            compiler_params=pltpu.CompilerParams(
                collective_id=0, has_side_effects=True, vmem_limit_bytes=40 * 1024 * 1024
            ),
        )(*[pltpu.with_memory_space_constraint(x, pltpu.HBM) for x in (tokens, weight, cotangent)])
        if C == 2:
            other = lax.ppermute(ig, "col", [(0, 1), (1, 0)])
            total = (ig.astype(F32) + other.astype(F32)).astype(BF)
        else:
            total = lax.psum(ig, "col")
        grad, act = weight_grad(dall.reshape(S * T, H), tall.reshape(S * T, F), act)
        return act, total, grad

    in_specs = (P("seq", "row"), P("row", "col"), P(("seq", "row"), "col"))
    out_specs = (P(("seq", "row"), "col"), P("seq", "row"), P(("col", "seq"), "row"))
    return jax.shard_map(shards, mesh=mesh, in_specs=in_specs, out_specs=out_specs, check_vma=False)
```
